32 devices in a mesh: lat: 8 (over z, x), fld: 4 (over y, core).
Axes of the slice: x: 2, y: 2, z: 4, core: 2. Of those that a mesh axis runs over, the one named last changes fastest.
Arguments:
- field_grid: bfloat16 [8, 2560, 5120], P('fld', 'lat'), may hold values from -300 to 300
- wave_table: int32 [64], replicated, may hold values from 0 to 1279, as said below
- legendre: bfloat16 [64, 2, 640, 1280], P('lat', None, 'fld'), may hold values from -0.15625 to 0.15625
Outputs:
- spectral: float32 [64, 640, 32], P('lat', 'fld')
The draws below stay inside these ranges and needn't reach their ends.
Inputs may be any that keep to these rules, and one draw needn't show every extreme that they name: `wave_table`: the entries differ from one another; each aligned block of 8 entries owned by one index of lat is made of pairs m and 1279 - m, next to each other.
All inputs are finite; a program needn't handle non-finite values.
Results may differ from the reference program's by a relative error of at most 0.0048.
Values may be sent and summed in bfloat16 or wider, within the bound.
A program may use at most 64 MiB of HBM per device.

```python
import math
import jax
import jax.numpy as jnp
from jax import lax

NLAT = 2560
NLON = 5120
TRUNC = 1280
FIELDS = 8
SLOTS = 64


def draw_wave_table(key, part):
    pair_count = TRUNC // 2
    chosen = jax.random.permutation(jax.random.fold_in(key, 11), pair_count - 1)[:SLOTS // 2 - 1] + 1
    chosen = jnp.concatenate([jnp.zeros((1,), jnp.int32), chosen.astype(jnp.int32)])
    chosen = jax.random.permutation(jax.random.fold_in(key, 12), chosen)
    paired = jnp.stack([chosen, TRUNC - 1 - chosen], axis=1)
    return paired.reshape(SLOTS).astype(jnp.int32)


def block_scale(key, dims, pieces, least, top_value):
    loudness = 1.0
    for dim, shards_of in pieces:
        steps = jax.random.uniform(jax.random.fold_in(jax.random.fold_in(key, 6), dim), (shards_of,), jnp.float32, least / len(pieces), top_value / len(pieces))
        loudness = loudness * jnp.repeat(jnp.exp(steps), dims[dim] // shards_of).reshape((-1,) + (1,) * (len(dims) - 1 - dim))
    return loudness


def noise(stream_key, extent, spread, most, shards=(), kind=jnp.bfloat16):
    drawn = jax.random.normal(stream_key, extent, jnp.float32) * spread
    if len(shards) > 0:
        drawn = block_scale(stream_key, extent, shards, -0.22, 0.18) * drawn
    return jnp.clip(drawn, min=-most, max=most).astype(kind)


def setup_inputs(seed: int = 0) -> dict:
    keys = jax.random.split(jax.random.key(seed), 4)
    return {
        "field_grid": noise(keys[0], (FIELDS, NLAT, NLON), 50.0, 300.0, ((0, 4), (1, 8))),
        "wave_table": draw_wave_table(jax.random.fold_in(keys[3], 71), 0),
        "legendre": noise(keys[2], (SLOTS, 2, TRUNC // 2, NLAT // 2), (NLAT // 2) ** -0.5, 0.15625, ((0, 8), (2, 4))),
    }


TWO_PI = 2.0 * math.pi


def twiddle_block(wave_block, lon_total):
    lon_index = jnp.arange(lon_total, dtype=jnp.int32)
    phase_index = (wave_block[:, None].astype(jnp.int32) * lon_index[None, :]) % lon_total
    angles = phase_index.astype(jnp.float32) * (TWO_PI / lon_total)
    cosine_sine = jnp.stack([jnp.cos(angles), -jnp.sin(angles)], axis=1)
    return cosine_sine.reshape(2 * wave_block.shape[0], lon_total).astype(jnp.bfloat16)


def fold_halves(fourier):
    half_lat = fourier.shape[-1] // 2
    north_rows = fourier[..., :half_lat].astype(jnp.float32)
    south_rows = jnp.flip(fourier[..., half_lat:], axis=-1).astype(jnp.float32)
    return jnp.stack([north_rows + south_rows, north_rows - south_rows], axis=1).astype(jnp.bfloat16)


def reference(field_grid, wave_table, legendre):
    grid_rows = field_grid.reshape(FIELDS * NLAT, NLON).astype(jnp.float32)
    block_size = math.gcd(SLOTS, 256)
    wave_blocks = wave_table.reshape(SLOTS // block_size, block_size)

    def transform(wave_block):
        twiddle = twiddle_block(wave_block, NLON).astype(jnp.float32)
        spectra = lax.dot_general(twiddle, grid_rows, (((1,), (1,)), ((), ())), precision=lax.Precision.HIGHEST, preferred_element_type=jnp.float32)
        return (spectra * (1.0 / NLON)).astype(jnp.bfloat16)

    fourier = lax.map(transform, wave_blocks).reshape(SLOTS, 2, FIELDS, NLAT)
    folded = fold_halves(fourier).reshape(SLOTS, 2, 2 * FIELDS, NLAT // 2)
    row_index = jnp.arange(TRUNC // 2, dtype=jnp.int32)
    parity = jnp.arange(2, dtype=jnp.int32)

    def contract(inputs):
        table_slot, folded_slot, wave = inputs
        coeffs = jnp.einsum("prj,pcj->rpc", table_slot.astype(jnp.float32), folded_slot.astype(jnp.float32), precision=lax.Precision.HIGHEST)
        degree = wave + 2 * row_index[:, None] + parity[None, :]
        valid_mask = (degree <= TRUNC - 1).astype(jnp.float32)
        return (coeffs * valid_mask[:, :, None]).reshape(TRUNC // 2, 4 * FIELDS)

    return lax.map(contract, (legendre, folded, wave_table))
```

```python
import functools
import math

import jax
import jax.numpy as jnp
from jax import lax
from jax.experimental import pallas as pl
from jax.experimental.pallas import tpu as pltpu
from jax.sharding import PartitionSpec as P

TWO_PI = 2.0 * math.pi


def twiddle_block(wave_block, lon_total):
    fine_count = math.gcd(lon_total, 128)
    coarse_count = lon_total // fine_count
    waves = wave_block[:, None]
    coarse_index = (
        waves * (jnp.arange(coarse_count, dtype=jnp.int32) * fine_count)[None, :] % lon_total
    )
    fine_index = waves * jnp.arange(fine_count, dtype=jnp.int32)[None, :] % lon_total
    coarse_angle = coarse_index.astype(jnp.float32) * (TWO_PI / lon_total)
    fine_angle = fine_index.astype(jnp.float32) * (TWO_PI / lon_total)
    coarse_cos = jnp.cos(coarse_angle)[:, :, None]
    coarse_sin = jnp.sin(coarse_angle)[:, :, None]
    fine_cos = jnp.cos(fine_angle)[:, None, :]
    fine_sin = jnp.sin(fine_angle)[:, None, :]
    cosine = (coarse_cos * fine_cos - coarse_sin * fine_sin).reshape(wave_block.shape[0], lon_total)
    minus_sine = (-(coarse_sin * fine_cos + coarse_cos * fine_sin)).reshape(
        wave_block.shape[0], lon_total
    )
    return jnp.concatenate([cosine, minus_sine], axis=0).astype(jnp.bfloat16)


def fold_halves(fourier):
    half_lat = fourier.shape[-1] // 2
    north_rows = fourier[..., :half_lat].astype(jnp.float32)
    south_rows = jnp.flip(fourier[..., half_lat:], axis=-1).astype(jnp.float32)
    return jnp.stack([north_rows + south_rows, north_rows - south_rows], axis=1).astype(
        jnp.bfloat16
    )


def shards_by_collectives(field_grid, wave_table, legendre):
    f_dev, lat_dev, lon_total = field_grid.shape
    slot_total = wave_table.shape[0]
    slot_dev = legendre.shape[0]
    row_dev = legendre.shape[2]
    grid_rows = field_grid.reshape(f_dev * lat_dev, lon_total)
    block_size = math.gcd(slot_total, 256)
    wave_blocks = wave_table.reshape(slot_total // block_size, block_size)

    def transform(wave_block):
        twiddle = twiddle_block(wave_block, lon_total)
        spectra = lax.dot_general(
            twiddle, grid_rows, (((1,), (1,)), ((), ())), preferred_element_type=jnp.float32
        )
        spectra = (spectra * (1.0 / lon_total)).astype(jnp.bfloat16)
        return jnp.transpose(spectra.reshape(2, block_size, f_dev, lat_dev), (1, 0, 2, 3))

    fourier = lax.map(transform, wave_blocks).reshape(slot_total, 2, f_dev, lat_dev)
    first_slot = lax.axis_index("lat") * slot_dev
    own_waves = lax.dynamic_slice_in_dim(wave_table, first_slot, slot_dev)
    trunc_total = 2 * row_dev * lax.axis_size("fld")
    row_index = lax.axis_index("fld") * row_dev + jnp.arange(row_dev, dtype=jnp.int32)
    parity = jnp.arange(2, dtype=jnp.int32)
    degree = own_waves[:, None, None] + 2 * row_index[None, :, None] + parity[None, None, :]
    valid_mask = (degree <= trunc_total - 1).astype(jnp.float32)
    regrouped = lax.all_to_all(fourier, "lat", split_axis=0, concat_axis=3, tiled=True)
    folded = fold_halves(regrouped)
    folded_piece = lax.all_gather(folded, "fld", axis=3, tiled=True)
    parts_count = folded_piece.shape[2]
    width = folded_piece.shape[3]
    merged = folded_piece.reshape(slot_dev, 2, parts_count * width, folded_piece.shape[4])
    coeffs = jnp.einsum("sprj,spcj->srpc", legendre, merged, preferred_element_type=jnp.float32)
    coeffs = coeffs.reshape(slot_dev, row_dev, 2, parts_count, width)
    coeffs = coeffs * valid_mask[:, :, :, None, None]
    return coeffs.reshape(slot_dev, row_dev, -1)


LANES = 128
HALF = 64
MESH = pl.DeviceIdType.MESH


def sin_cos_of_phase(phase, period):
    turns = jnp.floor(phase * (1.0 / period))
    rest = phase - turns * period
    rest = jnp.where(rest < 0, rest + period, rest)
    rest = jnp.where(rest >= period, rest - period, rest)
    eighth = period / 8
    q0 = rest < eighth
    q1 = rest < 3 * eighth
    q2 = rest < 5 * eighth
    q3 = rest < 7 * eighth
    centre = jnp.where(
        q0, 0.0, jnp.where(q1, 2 * eighth, jnp.where(q2, 4 * eighth, jnp.where(q3, 6 * eighth, period)))
    )
    x = (rest - centre) * (TWO_PI / period)
    y = x * x
    s = x * (1.0 + y * (-1 / 6 + y * (1 / 120 + y * (-1 / 5040 + y * (1 / 362880)))))
    c = 1.0 + y * (-1 / 2 + y * (1 / 24 + y * (-1 / 720 + y * (1 / 40320 - y * (1 / 3628800)))))
    even = q0 | (q2 & ~q1) | ~q3
    minus_sin = (q3 & ~q1)
    minus_cos = (q2 & ~q0)
    sine = jnp.where(even, s, c)
    sine = jnp.where(minus_sin, -sine, sine)
    cosine = jnp.where(even, c, s)
    cosine = jnp.where(minus_cos, -cosine, cosine)
    return sine, cosine


def transform_kernel(
    lat_count, wave_scalar_ref, wave_row_ref, field_ref, legendre_ref, out_ref,
    grid, twiddle, coarse, table, send, recv, folded, spun,
    field_sem, table_sem, send_sem, recv_sem, y_send, y_recv, c_send, c_recv, d_send, d_recv,
):
    lat = lax.axis_index("lat")
    fld = lax.axis_index("fld")
    y_peer = (fld + 2) % 4
    partner = fld + 1 - 2 * (fld % 2)
    partner_y = (partner + 2) % 4

    _, lat_dev, lon_total = field_ref.shape
    main = lat_dev // LANES
    tiles = 2 * main + 1
    slot_dev, _, row_dev, _ = legendre_ref.shape
    slot_total = wave_row_ref.shape[1]
    half_lats = lat_count // 2

    south = lat // half_lats
    band = lat + south * (lat_count - 1 - 2 * lat)
    odd = band % 2
    mixed = (south + odd) % 2

    barrier = pltpu.get_barrier_semaphore()
    for d in range(1, lat_count):
        pl.semaphore_signal(
            barrier, inc=1, device_id=((lat + d) % lat_count, fld), device_id_type=MESH
        )
    for other in (y_peer, partner):
        pl.semaphore_signal(barrier, inc=1, device_id=(lat, other), device_id_type=MESH)

    loads = []

    def load(f, row, count, dst):
        k = len(loads)
        copy = pltpu.make_async_copy(
            field_ref.at[f, pl.ds(pl.multiple_of(row, HALF), count)],
            grid.at[pl.ds(pl.multiple_of(dst, HALF), count)],
            field_sem.at[k],
        )
        copy.start()
        loads.append(copy)

    def load_main(f, t, dst):
        north_row = LANES * t + HALF * odd
        south_row = lat_dev - LANES - LANES * t - HALF * odd
        load(f, north_row + south * (south_row - north_row), LANES, dst)

    for t in range(main):
        load_main(0, t, LANES * t)
    tail_row = (lat_dev - HALF) * (1 - mixed)
    load(0, tail_row, HALF, LANES * main + HALF * mixed)
    load(1, tail_row, HALF, LANES * main + HALF * (1 - mixed))
    for t in range(main):
        load_main(1, t, LANES * (main + 1 + t))

    waves = wave_row_ref[...].astype(jnp.float32)
    waves = jnp.concatenate([waves, waves], axis=1)
    width = 2 * slot_total
    coarse_count = lon_total // LANES
    k_fine = lax.broadcasted_iota(jnp.int32, (LANES, width), 0).astype(jnp.float32)
    is_sine = lax.broadcasted_iota(jnp.int32, (LANES, width), 1) >= slot_total
    quarter = jnp.where(is_sine, lon_total / 4, 0.0)
    fine_sin, fine_cos = sin_cos_of_phase(waves * k_fine + quarter, lon_total)
    coarse_rows = coarse.shape[1]
    k_coarse = lax.broadcasted_iota(jnp.int32, (coarse_rows, width), 0).astype(jnp.float32) * LANES
    coarse_sin, coarse_cos = sin_cos_of_phase(waves * k_coarse, lon_total)
    coarse[0] = coarse_sin
    coarse[1] = coarse_cos
    for a in range(coarse_count):
        block = coarse[1, pl.ds(a, 1), :] * fine_cos - coarse[0, pl.ds(a, 1), :] * fine_sin
        twiddle[pl.ds(a * LANES, LANES), :] = block.astype(jnp.bfloat16)

    row = lax.broadcasted_iota(jnp.int32, (LANES, LANES), 0)
    column = lax.broadcasted_iota(jnp.int32, (LANES, LANES), 1)
    turned = row + south * (LANES - 1 - 2 * row)
    order = (turned == column).astype(jnp.float32).astype(jnp.bfloat16)

    chunk_tiles = ((0, main), (main, tiles))
    chunk_loads = ((0, main), (main, len(loads)))
    offsets = [d for pair in zip(range(lat_count // 2, 0, -1), range(lat_count // 2, lat_count)) for d in pair]
    offsets = list(dict.fromkeys(offsets))

    def columns(q):
        low, high = chunk_tiles[q]
        return pl.ds(low * LANES, (high - low) * LANES)

    pending = []
    for q in range(2):
        for k in range(*chunk_loads[q]):
            loads[k].wait()
        low, high = chunk_tiles[q]
        spectra = jnp.dot(
            grid[pl.ds(low * LANES, (high - low) * LANES), :], twiddle[...],
            preferred_element_type=jnp.float32,
        )
        spectra = (spectra * (1.0 / lon_total)).astype(jnp.bfloat16)
        for t in range(low, high):
            part = spectra[(t - low) * LANES:(t - low + 1) * LANES, :]
            part = jnp.dot(order, part, preferred_element_type=jnp.float32)
            part = part.T
            for owner in range(lat_count):
                s0 = owner * slot_dev
                send[owner, :, pl.ds(t * LANES, LANES)] = jnp.concatenate(
                    [part[s0:s0 + slot_dev], part[slot_total + s0:slot_total + s0 + slot_dev]], axis=0
                ).astype(jnp.bfloat16)
        if q == 0:
            pl.semaphore_wait(barrier, lat_count + 1)
        for d in offsets:
            owner = (lat + d) % lat_count
            copy = pltpu.make_async_remote_copy(
                src_ref=send.at[owner, :, columns(q)],
                dst_ref=recv.at[fld, lat, :, columns(q)],
                send_sem=send_sem.at[d, q],
                recv_sem=recv_sem.at[d, q],
                device_id=(owner, fld),
                device_id_type=MESH,
            )
            copy.start()
            pending.append(copy)
        for other, ss, rs in ((y_peer, y_send, y_recv), (partner, c_send, c_recv)):
            copy = pltpu.make_async_remote_copy(
                src_ref=send.at[lat, :, columns(q)],
                dst_ref=recv.at[fld, lat, :, columns(q)],
                send_sem=ss.at[0, q],
                recv_sem=rs.at[0, q],
                device_id=(lat, other),
                device_id_type=MESH,
            )
            copy.start()
            pending.append(copy)
        recv[fld, lat, :, columns(q)] = send[lat, :, columns(q)]

    table_copy = pltpu.make_async_copy(legendre_ref, table, table_sem)
    table_copy.start()

    near = list(reversed(offsets))
    for q in range(2):
        for d in near:
            src = (lat + lat_count - d) % lat_count
            here = recv.at[fld, src, :, columns(q)]
            pltpu.make_async_remote_copy(
                src_ref=here, dst_ref=here, send_sem=send_sem.at[d, q], recv_sem=recv_sem.at[d, q],
                device_id=(lat, y_peer), device_id_type=MESH,
            ).wait_recv()
            for other, ss, rs in ((y_peer, y_send, y_recv), (partner, c_send, c_recv)):
                copy = pltpu.make_async_remote_copy(
                    src_ref=here, dst_ref=here, send_sem=ss.at[d, q], recv_sem=rs.at[d, q],
                    device_id=(lat, other), device_id_type=MESH,
                )
                copy.start()
                pending.append(copy)
        for d in [0] + near:
            src = (lat + lat_count - d) % lat_count
            there = recv.at[y_peer, src, :, columns(q)]
            pltpu.make_async_remote_copy(
                src_ref=there, dst_ref=there, send_sem=y_send.at[d, q], recv_sem=y_recv.at[d, q],
                device_id=(lat, y_peer), device_id_type=MESH,
            ).wait_recv()
            copy = pltpu.make_async_remote_copy(
                src_ref=there, dst_ref=there, send_sem=d_send.at[d, q], recv_sem=d_recv.at[d, q],
                device_id=(lat, partner), device_id_type=MESH,
            )
            copy.start()
            pending.append(copy)
    for q in range(2):
        for d in [0] + near:
            src = (lat + lat_count - d) % lat_count
            for group, ss, rs in ((partner, c_send, c_recv), (partner_y, d_send, d_recv)):
                place = recv.at[group, src, :, columns(q)]
                pltpu.make_async_remote_copy(
                    src_ref=place, dst_ref=place, send_sem=ss.at[d, q], recv_sem=rs.at[d, q],
                    device_id=(lat, partner), device_id_type=MESH,
                ).wait_recv()

    depth = 2 * slot_dev
    pair_lats = 2 * lat_dev
    low_half = lax.broadcasted_iota(jnp.int32, (depth, LANES), 1) < HALF
    for h in range(half_lats // 2):
        for group in range(4):
            north = [recv[group, 2 * h + o].astype(jnp.float32) for o in range(2)]
            mirror = [recv[group, lat_count - 1 - 2 * h - o].astype(jnp.float32) for o in range(2)]
            for p in range(2):
                even_band, odd_band = [
                    n + m if p == 0 else n - m for n, m in zip(north, mirror)
                ]
                cut = main * LANES
                mid_even = even_band[:, cut:cut + LANES]
                mid_odd = odd_band[:, cut:cut + LANES]
                mid = (
                    jnp.where(low_half, mid_even, mid_odd),
                    pltpu.roll(jnp.where(low_half, mid_odd, mid_even), HALF, 1),
                )
                for f in range(2):
                    start = f * (cut + LANES)
                    rows = pl.ds((2 * group + f) * depth, depth)
                    base = h * pair_lats
                    folded[p, rows, pl.ds(base, cut)] = even_band[:, start:start + cut].astype(jnp.bfloat16)
                    folded[p, rows, pl.ds(base + cut, LANES)] = mid[f].astype(jnp.bfloat16)
                    folded[p, rows, pl.ds(base + cut + LANES, cut)] = odd_band[
                        :, start:start + cut
                    ].astype(jnp.bfloat16)

    table_copy.wait()
    total_rows = 8 * depth
    trunc_total = 2 * row_dev * 4
    slot_of = lax.broadcasted_iota(jnp.int32, (row_dev, total_rows), 1) % slot_dev
    degree_row = 2 * (lax.broadcasted_iota(jnp.int32, (row_dev, total_rows), 0) + fld * row_dev)
    for p in range(2):
        kept = jnp.zeros((row_dev, total_rows), jnp.float32)
        for s in range(slot_dev):
            sums = lax.dot_general(
                table[s, p], folded[p], (((1,), (1,)), ((), ())), preferred_element_type=jnp.float32
            )
            wave = wave_scalar_ref[lat * slot_dev + s]
            valid = (slot_of == s) & (degree_row + (wave + p) <= trunc_total - 1)
            kept = jnp.where(valid, sums, kept)
        padded = jnp.concatenate(
            [kept, jnp.zeros((spun.shape[1] * LANES - row_dev, total_rows), jnp.float32)], axis=0
        )
        for t in range(spun.shape[1]):
            spun[p, t] = padded[t * LANES:(t + 1) * LANES].T
    for s in range(slot_dev):
        for p in range(2):
            for c in range(2):
                for t in range(spun.shape[1]):
                    kept_rows = min(LANES, row_dev - t * LANES)
                    out_ref[s, pl.ds(p * 16 + c * 8, 8), pl.ds(t * LANES, kept_rows)] = spun[
                        p, t, pl.ds(c * slot_dev + s, 8, stride=depth), :
                    ][:, :kept_rows]
    for copy in pending:
        copy.wait_send()


def shards_by_kernel(field_grid, wave_table, legendre):
    f_dev, lat_dev, lon_total = field_grid.shape
    slot_dev, _, row_dev, north_total = legendre.shape
    slot_total = wave_table.shape[0]
    lat_count = lax.axis_size("lat")
    rows = f_dev * lat_dev
    bf16, f32 = jnp.bfloat16, jnp.float32
    dma = pltpu.SemaphoreType.DMA
    padded_rows = -(-row_dev // LANES) * LANES
    coarse_rows = -(-(lon_total // LANES) // 8) * 8
    vmem, smem = pltpu.VMEM, pltpu.SMEM
    pairs = (lat_count, 2)
    out = pl.pallas_call(
        functools.partial(transform_kernel, lat_count),
        out_shape=jax.ShapeDtypeStruct((slot_dev, 32, row_dev), f32),
        in_specs=[
            pl.BlockSpec(memory_space=smem),
            pl.BlockSpec(memory_space=vmem),
            pl.BlockSpec(memory_space=pl.ANY),
            pl.BlockSpec(memory_space=pl.ANY),
        ],
        out_specs=pl.BlockSpec(memory_space=vmem),
        scratch_shapes=[
            vmem((rows, lon_total), bf16),
            vmem((lon_total, 2 * slot_total), bf16),
            vmem((2, coarse_rows, 2 * slot_total), f32),
            vmem(legendre.shape, bf16),
            vmem((lat_count, 2 * slot_dev, rows), bf16),
            vmem((4, lat_count, 2 * slot_dev, rows), bf16),
            vmem((2, 16 * slot_dev, north_total), bf16),
            vmem((2, padded_rows // LANES, 16 * slot_dev, LANES), f32),
            dma((2 * (lat_dev // LANES) + 2,)),
            dma(()),
        ] + [dma(pairs)] * 8,
        compiler_params=pltpu.CompilerParams(
            collective_id=0, has_side_effects=True
        ),
    )(wave_table, wave_table.reshape(1, slot_total), field_grid, legendre)
    return jnp.transpose(out, (0, 2, 1))


def shards(field_grid, wave_table, legendre):
    f_dev, lat_dev, lon_total = field_grid.shape
    slot_dev, _, row_dev, _ = legendre.shape
    slot_total = wave_table.shape[0]
    fits = (
        f_dev == 2
        and slot_dev == 8
        and 2 * slot_total == LANES
        and lat_dev % LANES == HALF
        and lax.axis_size("fld") == 4
        and lax.axis_size("lat") % 4 == 0
        and lon_total % LANES == 0
        and row_dev % 8 == 0
        and 2 * row_dev * 4 * lon_total < 2**24
    )
    if fits:
        return shards_by_kernel(field_grid, wave_table, legendre)
    return shards_by_collectives(field_grid, wave_table, legendre)


def solution(mesh):
    placed = (P("fld", "lat", None), P(), P("lat", None, "fld", None))
    return jax.shard_map(
        shards, mesh=mesh, in_specs=placed, out_specs=P("lat", "fld", None), check_vma=False
    )
```

```python
import functools
import math

import jax
import jax.numpy as jnp
from jax import lax
from jax.experimental import pallas as pl
from jax.experimental.pallas import tpu as pltpu
from jax.sharding import PartitionSpec as P

TWO_PI = 2.0 * math.pi


def twiddle_block(wave_block, lon_total):
    fine_count = math.gcd(lon_total, 128)
    coarse_count = lon_total // fine_count
    waves = wave_block[:, None]
    coarse_index = (
        waves * (jnp.arange(coarse_count, dtype=jnp.int32) * fine_count)[None, :] % lon_total
    )
    fine_index = waves * jnp.arange(fine_count, dtype=jnp.int32)[None, :] % lon_total
    coarse_angle = coarse_index.astype(jnp.float32) * (TWO_PI / lon_total)
    fine_angle = fine_index.astype(jnp.float32) * (TWO_PI / lon_total)
    coarse_cos = jnp.cos(coarse_angle)[:, :, None]
    coarse_sin = jnp.sin(coarse_angle)[:, :, None]
    fine_cos = jnp.cos(fine_angle)[:, None, :]
    fine_sin = jnp.sin(fine_angle)[:, None, :]
    cosine = (coarse_cos * fine_cos - coarse_sin * fine_sin).reshape(wave_block.shape[0], lon_total)
    minus_sine = (-(coarse_sin * fine_cos + coarse_cos * fine_sin)).reshape(
        wave_block.shape[0], lon_total
    )
    return jnp.concatenate([cosine, minus_sine], axis=0).astype(jnp.bfloat16)


def fold_halves(fourier):
    half_lat = fourier.shape[-1] // 2
    north_rows = fourier[..., :half_lat].astype(jnp.float32)
    south_rows = jnp.flip(fourier[..., half_lat:], axis=-1).astype(jnp.float32)
    return jnp.stack([north_rows + south_rows, north_rows - south_rows], axis=1).astype(
        jnp.bfloat16
    )


def shards_by_collectives(field_grid, wave_table, legendre):
    f_dev, lat_dev, lon_total = field_grid.shape
    slot_total = wave_table.shape[0]
    slot_dev = legendre.shape[0]
    row_dev = legendre.shape[2]
    grid_rows = field_grid.reshape(f_dev * lat_dev, lon_total)
    block_size = math.gcd(slot_total, 256)
    wave_blocks = wave_table.reshape(slot_total // block_size, block_size)

    def transform(wave_block):
        twiddle = twiddle_block(wave_block, lon_total)
        spectra = lax.dot_general(
            twiddle, grid_rows, (((1,), (1,)), ((), ())), preferred_element_type=jnp.float32
        )
        spectra = (spectra * (1.0 / lon_total)).astype(jnp.bfloat16)
        return jnp.transpose(spectra.reshape(2, block_size, f_dev, lat_dev), (1, 0, 2, 3))

    fourier = lax.map(transform, wave_blocks).reshape(slot_total, 2, f_dev, lat_dev)
    first_slot = lax.axis_index("lat") * slot_dev
    own_waves = lax.dynamic_slice_in_dim(wave_table, first_slot, slot_dev)
    trunc_total = 2 * row_dev * lax.axis_size("fld")
    row_index = lax.axis_index("fld") * row_dev + jnp.arange(row_dev, dtype=jnp.int32)
    parity = jnp.arange(2, dtype=jnp.int32)
    degree = own_waves[:, None, None] + 2 * row_index[None, :, None] + parity[None, None, :]
    valid_mask = (degree <= trunc_total - 1).astype(jnp.float32)
    regrouped = lax.all_to_all(fourier, "lat", split_axis=0, concat_axis=3, tiled=True)
    folded = fold_halves(regrouped)
    folded_piece = lax.all_gather(folded, "fld", axis=3, tiled=True)
    parts_count = folded_piece.shape[2]
    width = folded_piece.shape[3]
    merged = folded_piece.reshape(slot_dev, 2, parts_count * width, folded_piece.shape[4])
    coeffs = jnp.einsum("sprj,spcj->srpc", legendre, merged, preferred_element_type=jnp.float32)
    coeffs = coeffs.reshape(slot_dev, row_dev, 2, parts_count, width)
    coeffs = coeffs * valid_mask[:, :, :, None, None]
    return coeffs.reshape(slot_dev, row_dev, -1)


LANES = 128
HALF = 64
MESH = pl.DeviceIdType.MESH


def sin_cos_of_phase(phase, period):
    turns = jnp.floor(phase * (1.0 / period))
    rest = phase - turns * period
    rest = jnp.where(rest < 0, rest + period, rest)
    rest = jnp.where(rest >= period, rest - period, rest)
    eighth = period / 8
    q0 = rest < eighth
    q1 = rest < 3 * eighth
    q2 = rest < 5 * eighth
    q3 = rest < 7 * eighth
    centre = jnp.where(
        q0, 0.0, jnp.where(q1, 2 * eighth, jnp.where(q2, 4 * eighth, jnp.where(q3, 6 * eighth, period)))
    )
    x = (rest - centre) * (TWO_PI / period)
    y = x * x
    s = x * (1.0 + y * (-1 / 6 + y * (1 / 120 + y * (-1 / 5040 + y * (1 / 362880)))))
    c = 1.0 + y * (-1 / 2 + y * (1 / 24 + y * (-1 / 720 + y * (1 / 40320 - y * (1 / 3628800)))))
    even = q0 | (q2 & ~q1) | ~q3
    minus_sin = (q3 & ~q1)
    minus_cos = (q2 & ~q0)
    sine = jnp.where(even, s, c)
    sine = jnp.where(minus_sin, -sine, sine)
    cosine = jnp.where(even, c, s)
    cosine = jnp.where(minus_cos, -cosine, cosine)
    return sine, cosine


def transform_kernel(
    lat_count, wave_scalar_ref, wave_row_ref, field_ref, legendre_ref, out_ref,
    grid, twiddle, coarse, table, send, recv, folded, spun,
    field_sem, table_sem, send_sem, recv_sem, y_send, y_recv, c_send, c_recv, d_send, d_recv,
):
    lat = lax.axis_index("lat")
    fld = lax.axis_index("fld")
    y_peer = (fld + 2) % 4
    partner = fld + 1 - 2 * (fld % 2)
    partner_y = (partner + 2) % 4

    _, lat_dev, lon_total = field_ref.shape
    main = lat_dev // LANES
    tiles = 2 * main + 1
    slot_dev, _, row_dev, _ = legendre_ref.shape
    slot_total = wave_row_ref.shape[1]
    half_lats = lat_count // 2

    south = lat // half_lats
    band = lat + south * (lat_count - 1 - 2 * lat)
    odd = band % 2
    mixed = (south + odd) % 2

    barrier = pltpu.get_barrier_semaphore()
    for d in range(1, lat_count):
        pl.semaphore_signal(
            barrier, inc=1, device_id=((lat + d) % lat_count, fld), device_id_type=MESH
        )
    for other in (y_peer, partner):
        pl.semaphore_signal(barrier, inc=1, device_id=(lat, other), device_id_type=MESH)

    loads = []

    def load(f, row, count, dst):
        k = len(loads)
        copy = pltpu.make_async_copy(
            field_ref.at[f, pl.ds(pl.multiple_of(row, HALF), count)],
            grid.at[pl.ds(pl.multiple_of(dst, HALF), count)],
            field_sem.at[k],
        )
        copy.start()
        loads.append(copy)

    def load_main(f, t, dst):
        north_row = LANES * t + HALF * odd
        south_row = lat_dev - LANES - LANES * t - HALF * odd
        load(f, north_row + south * (south_row - north_row), LANES, dst)

    for t in range(main):
        load_main(0, t, LANES * t)
    tail_row = (lat_dev - HALF) * (1 - mixed)
    load(0, tail_row, HALF, LANES * main + HALF * mixed)
    load(1, tail_row, HALF, LANES * main + HALF * (1 - mixed))
    for t in range(main):
        load_main(1, t, LANES * (main + 1 + t))

    waves = wave_row_ref[...].astype(jnp.float32)
    waves = jnp.concatenate([waves, waves], axis=1)
    width = 2 * slot_total
    coarse_count = lon_total // LANES
    k_fine = lax.broadcasted_iota(jnp.int32, (LANES, width), 0).astype(jnp.float32)
    is_sine = lax.broadcasted_iota(jnp.int32, (LANES, width), 1) >= slot_total
    quarter = jnp.where(is_sine, lon_total / 4, 0.0)
    fine_sin, fine_cos = sin_cos_of_phase(waves * k_fine + quarter, lon_total)
    coarse_rows = coarse.shape[1]
    k_coarse = lax.broadcasted_iota(jnp.int32, (coarse_rows, width), 0).astype(jnp.float32) * LANES
    coarse_sin, coarse_cos = sin_cos_of_phase(waves * k_coarse, lon_total)
    coarse[0] = coarse_sin
    coarse[1] = coarse_cos
    for a in range(coarse_count):
        block = coarse[1, pl.ds(a, 1), :] * fine_cos - coarse[0, pl.ds(a, 1), :] * fine_sin
        twiddle[pl.ds(a * LANES, LANES), :] = block.astype(jnp.bfloat16)

    row = lax.broadcasted_iota(jnp.int32, (LANES, LANES), 0)
    column = lax.broadcasted_iota(jnp.int32, (LANES, LANES), 1)
    turned = row + south * (LANES - 1 - 2 * row)
    order = (turned == column).astype(jnp.float32).astype(jnp.bfloat16)

    chunk_tiles = ((0, main), (main, tiles))
    chunk_loads = ((0, main), (main, len(loads)))
    near = sorted(range(1, lat_count))
    offsets = near[::-1]

    def flipped(d):
        index, bit = lat, 1
        while bit < lat_count:
            if d & bit:
                index = index + bit * (1 - 2 * ((lat // bit) % 2))
            bit *= 2
        return index

    def columns(q):
        low, high = chunk_tiles[q]
        return pl.ds(low * LANES, (high - low) * LANES)

    pending = []
    for q in range(2):
        for k in range(*chunk_loads[q]):
            loads[k].wait()
        low, high = chunk_tiles[q]
        spectra = jnp.dot(
            grid[pl.ds(low * LANES, (high - low) * LANES), :], twiddle[...],
            preferred_element_type=jnp.float32,
        )
        spectra = (spectra * (1.0 / lon_total)).astype(jnp.bfloat16)
        for t in range(low, high):
            part = spectra[(t - low) * LANES:(t - low + 1) * LANES, :]
            part = jnp.dot(order, part, preferred_element_type=jnp.float32)
            part = part.T
            for owner in range(lat_count):
                s0 = owner * slot_dev
                send[owner, :, pl.ds(t * LANES, LANES)] = jnp.concatenate(
                    [part[s0:s0 + slot_dev], part[slot_total + s0:slot_total + s0 + slot_dev]], axis=0
                ).astype(jnp.bfloat16)
        if q == 0:
            pl.semaphore_wait(barrier, lat_count + 1)
        for d in offsets:
            owner = flipped(d)
            copy = pltpu.make_async_remote_copy(
                src_ref=send.at[owner, :, columns(q)],
                dst_ref=recv.at[fld, lat, :, columns(q)],
                send_sem=send_sem.at[d, q],
                recv_sem=recv_sem.at[d, q],
                device_id=(owner, fld),
                device_id_type=MESH,
            )
            copy.start()
            pending.append(copy)
        for other, ss, rs in ((y_peer, y_send, y_recv), (partner, c_send, c_recv)):
            copy = pltpu.make_async_remote_copy(
                src_ref=send.at[lat, :, columns(q)],
                dst_ref=recv.at[fld, lat, :, columns(q)],
                send_sem=ss.at[0, q],
                recv_sem=rs.at[0, q],
                device_id=(lat, other),
                device_id_type=MESH,
            )
            copy.start()
            pending.append(copy)
        recv[fld, lat, :, columns(q)] = send[lat, :, columns(q)]

    table_copy = pltpu.make_async_copy(legendre_ref, table, table_sem)
    table_copy.start()

    for q in range(2):
        for d in near:
            src = flipped(d)
            here = recv.at[fld, src, :, columns(q)]
            pltpu.make_async_remote_copy(
                src_ref=here, dst_ref=here, send_sem=send_sem.at[d, q], recv_sem=recv_sem.at[d, q],
                device_id=(lat, y_peer), device_id_type=MESH,
            ).wait_recv()
            for other, ss, rs in ((y_peer, y_send, y_recv), (partner, c_send, c_recv)):
                copy = pltpu.make_async_remote_copy(
                    src_ref=here, dst_ref=here, send_sem=ss.at[d, q], recv_sem=rs.at[d, q],
                    device_id=(lat, other), device_id_type=MESH,
                )
                copy.start()
                pending.append(copy)
    for q in range(2):
        for d in [0] + near:
            src = flipped(d)
            there = recv.at[y_peer, src, :, columns(q)]
            pltpu.make_async_remote_copy(
                src_ref=there, dst_ref=there, send_sem=y_send.at[d, q], recv_sem=y_recv.at[d, q],
                device_id=(lat, y_peer), device_id_type=MESH,
            ).wait_recv()
            copy = pltpu.make_async_remote_copy(
                src_ref=there, dst_ref=there, send_sem=d_send.at[d, q], recv_sem=d_recv.at[d, q],
                device_id=(lat, partner), device_id_type=MESH,
            )
            copy.start()
            pending.append(copy)
    for q in range(2):
        for d in [0] + near:
            src = flipped(d)
            for group, ss, rs in ((partner, c_send, c_recv), (partner_y, d_send, d_recv)):
                place = recv.at[group, src, :, columns(q)]
                pltpu.make_async_remote_copy(
                    src_ref=place, dst_ref=place, send_sem=ss.at[d, q], recv_sem=rs.at[d, q],
                    device_id=(lat, partner), device_id_type=MESH,
                ).wait_recv()

    depth = 2 * slot_dev
    pair_lats = 2 * lat_dev
    low_half = lax.broadcasted_iota(jnp.int32, (depth, LANES), 1) < HALF
    for h in range(half_lats // 2):
        for group in range(4):
            north = [recv[group, 2 * h + o].astype(jnp.float32) for o in range(2)]
            mirror = [recv[group, lat_count - 1 - 2 * h - o].astype(jnp.float32) for o in range(2)]
            for p in range(2):
                even_band, odd_band = [
                    n + m if p == 0 else n - m for n, m in zip(north, mirror)
                ]
                cut = main * LANES
                mid_even = even_band[:, cut:cut + LANES]
                mid_odd = odd_band[:, cut:cut + LANES]
                mid = (
                    jnp.where(low_half, mid_even, mid_odd),
                    pltpu.roll(jnp.where(low_half, mid_odd, mid_even), HALF, 1),
                )
                for f in range(2):
                    start = f * (cut + LANES)
                    rows = pl.ds((2 * group + f) * depth, depth)
                    base = h * pair_lats
                    folded[p, rows, pl.ds(base, cut)] = even_band[:, start:start + cut].astype(jnp.bfloat16)
                    folded[p, rows, pl.ds(base + cut, LANES)] = mid[f].astype(jnp.bfloat16)
                    folded[p, rows, pl.ds(base + cut + LANES, cut)] = odd_band[
                        :, start:start + cut
                    ].astype(jnp.bfloat16)

    table_copy.wait()
    total_rows = 8 * depth
    trunc_total = 2 * row_dev * 4
    slot_of = lax.broadcasted_iota(jnp.int32, (row_dev, total_rows), 1) % slot_dev
    degree_row = 2 * (lax.broadcasted_iota(jnp.int32, (row_dev, total_rows), 0) + fld * row_dev)
    for p in range(2):
        kept = jnp.zeros((row_dev, total_rows), jnp.float32)
        for s in range(slot_dev):
            sums = lax.dot_general(
                table[s, p], folded[p], (((1,), (1,)), ((), ())), preferred_element_type=jnp.float32
            )
            wave = wave_scalar_ref[lat * slot_dev + s]
            valid = (slot_of == s) & (degree_row + (wave + p) <= trunc_total - 1)
            kept = jnp.where(valid, sums, kept)
        padded = jnp.concatenate(
            [kept, jnp.zeros((spun.shape[1] * LANES - row_dev, total_rows), jnp.float32)], axis=0
        )
        for t in range(spun.shape[1]):
            spun[p, t] = padded[t * LANES:(t + 1) * LANES].T
    for s in range(slot_dev):
        for p in range(2):
            for c in range(2):
                for t in range(spun.shape[1]):
                    kept_rows = min(LANES, row_dev - t * LANES)
                    out_ref[s, pl.ds(p * 16 + c * 8, 8), pl.ds(t * LANES, kept_rows)] = spun[
                        p, t, pl.ds(c * slot_dev + s, 8, stride=depth), :
                    ][:, :kept_rows]
    for copy in pending:
        copy.wait_send()


def shards_by_kernel(field_grid, wave_table, legendre):
    f_dev, lat_dev, lon_total = field_grid.shape
    slot_dev, _, row_dev, north_total = legendre.shape
    slot_total = wave_table.shape[0]
    lat_count = lax.axis_size("lat")
    rows = f_dev * lat_dev
    bf16, f32 = jnp.bfloat16, jnp.float32
    dma = pltpu.SemaphoreType.DMA
    padded_rows = -(-row_dev // LANES) * LANES
    coarse_rows = -(-(lon_total // LANES) // 8) * 8
    vmem, smem = pltpu.VMEM, pltpu.SMEM
    pairs = (lat_count, 2)
    out = pl.pallas_call(
        functools.partial(transform_kernel, lat_count),
        out_shape=pltpu.VMEM((slot_dev, 32, row_dev), f32),
        in_specs=[
            pl.BlockSpec(memory_space=smem),
            pl.BlockSpec(memory_space=vmem),
            pl.BlockSpec(memory_space=pl.ANY),
            pl.BlockSpec(memory_space=pl.ANY),
        ],
        out_specs=pl.BlockSpec(memory_space=vmem),
        scratch_shapes=[
            vmem((rows, lon_total), bf16),
            vmem((lon_total, 2 * slot_total), bf16),
            vmem((2, coarse_rows, 2 * slot_total), f32),
            vmem(legendre.shape, bf16),
            vmem((lat_count, 2 * slot_dev, rows), bf16),
            vmem((4, lat_count, 2 * slot_dev, rows), bf16),
            vmem((2, 16 * slot_dev, north_total), bf16),
            vmem((2, padded_rows // LANES, 16 * slot_dev, LANES), f32),
            dma((2 * (lat_dev // LANES) + 2,)),
            dma(()),
        ] + [dma(pairs)] * 8,
        compiler_params=pltpu.CompilerParams(
            collective_id=0, has_side_effects=True
        ),
    )(wave_table, wave_table.reshape(1, slot_total), field_grid, legendre)
    return jnp.transpose(out, (0, 2, 1))


def shards(field_grid, wave_table, legendre):
    f_dev, lat_dev, lon_total = field_grid.shape
    slot_dev, _, row_dev, _ = legendre.shape
    slot_total = wave_table.shape[0]
    fits = (
        f_dev == 2
        and slot_dev == 8
        and 2 * slot_total == LANES
        and lat_dev % LANES == HALF
        and lax.axis_size("fld") == 4
        and lax.axis_size("lat") in (4, 8, 16)
        and lon_total % LANES == 0
        and row_dev % 8 == 0
        and 2 * row_dev * 4 * lon_total < 2**24
    )
    if fits:
        return shards_by_kernel(field_grid, wave_table, legendre)
    return shards_by_collectives(field_grid, wave_table, legendre)


def solution(mesh):
    placed = (P("fld", "lat", None), P(), P("lat", None, "fld", None))
    return jax.shard_map(
        shards, mesh=mesh, in_specs=placed, out_specs=P("lat", "fld", None), check_vma=False
    )
```

```python
import functools
import math

import jax
import jax.numpy as jnp
from jax import lax
from jax.experimental import pallas as pl
from jax.experimental.pallas import tpu as pltpu
from jax.sharding import PartitionSpec as P

TWO_PI = 2.0 * math.pi


def twiddle_block(wave_block, lon_total):
    fine_count = math.gcd(lon_total, 128)
    coarse_count = lon_total // fine_count
    waves = wave_block[:, None]
    coarse_index = (
        waves * (jnp.arange(coarse_count, dtype=jnp.int32) * fine_count)[None, :] % lon_total
    )
    fine_index = waves * jnp.arange(fine_count, dtype=jnp.int32)[None, :] % lon_total
    coarse_angle = coarse_index.astype(jnp.float32) * (TWO_PI / lon_total)
    fine_angle = fine_index.astype(jnp.float32) * (TWO_PI / lon_total)
    coarse_cos = jnp.cos(coarse_angle)[:, :, None]
    coarse_sin = jnp.sin(coarse_angle)[:, :, None]
    fine_cos = jnp.cos(fine_angle)[:, None, :]
    fine_sin = jnp.sin(fine_angle)[:, None, :]
    cosine = (coarse_cos * fine_cos - coarse_sin * fine_sin).reshape(wave_block.shape[0], lon_total)
    minus_sine = (-(coarse_sin * fine_cos + coarse_cos * fine_sin)).reshape(
        wave_block.shape[0], lon_total
    )
    return jnp.concatenate([cosine, minus_sine], axis=0).astype(jnp.bfloat16)


def fold_halves(fourier):
    half_lat = fourier.shape[-1] // 2
    north_rows = fourier[..., :half_lat].astype(jnp.float32)
    south_rows = jnp.flip(fourier[..., half_lat:], axis=-1).astype(jnp.float32)
    return jnp.stack([north_rows + south_rows, north_rows - south_rows], axis=1).astype(
        jnp.bfloat16
    )


def shards_by_collectives(field_grid, wave_table, legendre):
    f_dev, lat_dev, lon_total = field_grid.shape
    slot_total = wave_table.shape[0]
    slot_dev = legendre.shape[0]
    row_dev = legendre.shape[2]
    grid_rows = field_grid.reshape(f_dev * lat_dev, lon_total)
    block_size = math.gcd(slot_total, 256)
    wave_blocks = wave_table.reshape(slot_total // block_size, block_size)

    def transform(wave_block):
        twiddle = twiddle_block(wave_block, lon_total)
        spectra = lax.dot_general(
            twiddle, grid_rows, (((1,), (1,)), ((), ())), preferred_element_type=jnp.float32
        )
        spectra = (spectra * (1.0 / lon_total)).astype(jnp.bfloat16)
        return jnp.transpose(spectra.reshape(2, block_size, f_dev, lat_dev), (1, 0, 2, 3))

    fourier = lax.map(transform, wave_blocks).reshape(slot_total, 2, f_dev, lat_dev)
    first_slot = lax.axis_index("lat") * slot_dev
    own_waves = lax.dynamic_slice_in_dim(wave_table, first_slot, slot_dev)
    trunc_total = 2 * row_dev * lax.axis_size("fld")
    row_index = lax.axis_index("fld") * row_dev + jnp.arange(row_dev, dtype=jnp.int32)
    parity = jnp.arange(2, dtype=jnp.int32)
    degree = own_waves[:, None, None] + 2 * row_index[None, :, None] + parity[None, None, :]
    valid_mask = (degree <= trunc_total - 1).astype(jnp.float32)
    regrouped = lax.all_to_all(fourier, "lat", split_axis=0, concat_axis=3, tiled=True)
    folded = fold_halves(regrouped)
    folded_piece = lax.all_gather(folded, "fld", axis=3, tiled=True)
    parts_count = folded_piece.shape[2]
    width = folded_piece.shape[3]
    merged = folded_piece.reshape(slot_dev, 2, parts_count * width, folded_piece.shape[4])
    coeffs = jnp.einsum("sprj,spcj->srpc", legendre, merged, preferred_element_type=jnp.float32)
    coeffs = coeffs.reshape(slot_dev, row_dev, 2, parts_count, width)
    coeffs = coeffs * valid_mask[:, :, :, None, None]
    return coeffs.reshape(slot_dev, row_dev, -1)


LANES = 128
HALF = 64
MESH = pl.DeviceIdType.MESH


def sin_cos_of_phase(phase, period):
    turns = jnp.floor(phase * (1.0 / period))
    rest = phase - turns * period
    rest = jnp.where(rest < 0, rest + period, rest)
    rest = jnp.where(rest >= period, rest - period, rest)
    eighth = period / 8
    q0 = rest < eighth
    q1 = rest < 3 * eighth
    q2 = rest < 5 * eighth
    q3 = rest < 7 * eighth
    centre = jnp.where(
        q0, 0.0, jnp.where(q1, 2 * eighth, jnp.where(q2, 4 * eighth, jnp.where(q3, 6 * eighth, period)))
    )
    x = (rest - centre) * (TWO_PI / period)
    y = x * x
    s = x * (1.0 + y * (-1 / 6 + y * (1 / 120 + y * (-1 / 5040 + y * (1 / 362880)))))
    c = 1.0 + y * (-1 / 2 + y * (1 / 24 + y * (-1 / 720 + y * (1 / 40320 - y * (1 / 3628800)))))
    even = q0 | (q2 & ~q1) | ~q3
    minus_sin = (q3 & ~q1)
    minus_cos = (q2 & ~q0)
    sine = jnp.where(even, s, c)
    sine = jnp.where(minus_sin, -sine, sine)
    cosine = jnp.where(even, c, s)
    cosine = jnp.where(minus_cos, -cosine, cosine)
    return sine, cosine


def transform_kernel(
    lat_count, wave_scalar_ref, wave_row_ref, field_ref, legendre_ref, out_ref,
    grid, twiddle, coarse, table, send, recv, folded, spun,
    field_sem, table_sem, send_sem, recv_sem, y_send, y_recv, c_send, c_recv, d_send, d_recv,
):
    lat = lax.axis_index("lat")
    fld = lax.axis_index("fld")
    y_peer = (fld + 2) % 4
    partner = fld + 1 - 2 * (fld % 2)
    partner_y = (partner + 2) % 4

    _, lat_dev, lon_total = field_ref.shape
    main = lat_dev // LANES
    tiles = 2 * main + 1
    slot_dev, _, row_dev, _ = legendre_ref.shape
    slot_total = wave_row_ref.shape[1]
    half_lats = lat_count // 2

    south = lat // half_lats
    band = lat + south * (lat_count - 1 - 2 * lat)
    odd = band % 2
    mixed = (south + odd) % 2

    barrier = pltpu.get_barrier_semaphore()
    for d in range(1, lat_count):
        pl.semaphore_signal(
            barrier, inc=1, device_id=((lat + d) % lat_count, fld), device_id_type=MESH
        )
    for other in (y_peer, partner):
        pl.semaphore_signal(barrier, inc=1, device_id=(lat, other), device_id_type=MESH)

    loads = []

    def load(f, row, count, dst):
        k = len(loads)
        copy = pltpu.make_async_copy(
            field_ref.at[f, pl.ds(pl.multiple_of(row, HALF), count)],
            grid.at[pl.ds(pl.multiple_of(dst, HALF), count)],
            field_sem.at[k],
        )
        copy.start()
        loads.append(copy)

    def load_main(f, t, dst):
        north_row = LANES * t + HALF * odd
        south_row = lat_dev - LANES - LANES * t - HALF * odd
        load(f, north_row + south * (south_row - north_row), LANES, dst)

    for t in range(main):
        load_main(0, t, LANES * t)
    tail_row = (lat_dev - HALF) * (1 - mixed)
    load(0, tail_row, HALF, LANES * main + HALF * mixed)
    load(1, tail_row, HALF, LANES * main + HALF * (1 - mixed))
    for t in range(main):
        load_main(1, t, LANES * (main + 1 + t))

    waves = wave_row_ref[...].astype(jnp.float32)
    waves = jnp.concatenate([waves, waves], axis=1)
    width = 2 * slot_total
    coarse_count = lon_total // LANES
    k_fine = lax.broadcasted_iota(jnp.int32, (LANES, width), 0).astype(jnp.float32)
    is_sine = lax.broadcasted_iota(jnp.int32, (LANES, width), 1) >= slot_total
    quarter = jnp.where(is_sine, lon_total / 4, 0.0)
    fine_sin, fine_cos = sin_cos_of_phase(waves * k_fine + quarter, lon_total)
    coarse_rows = coarse.shape[1]
    k_coarse = lax.broadcasted_iota(jnp.int32, (coarse_rows, width), 0).astype(jnp.float32) * LANES
    coarse_sin, coarse_cos = sin_cos_of_phase(waves * k_coarse, lon_total)
    coarse[0] = coarse_sin
    coarse[1] = coarse_cos
    for a in range(coarse_count):
        block = coarse[1, pl.ds(a, 1), :] * fine_cos - coarse[0, pl.ds(a, 1), :] * fine_sin
        twiddle[pl.ds(a * LANES, LANES), :] = block.astype(jnp.bfloat16)

    row = lax.broadcasted_iota(jnp.int32, (LANES, LANES), 0)
    column = lax.broadcasted_iota(jnp.int32, (LANES, LANES), 1)
    turned = row + south * (LANES - 1 - 2 * row)
    order = (turned == column).astype(jnp.float32).astype(jnp.bfloat16)

    chunk_tiles = ((0, main), (main, main + 1), (main + 1, tiles))
    chunk_loads = ((0, main), (main, main + 2), (main + 2, len(loads)))
    near = sorted(range(1, lat_count))
    offsets = near[::-1]

    def flipped(d):
        index, bit = lat, 1
        while bit < lat_count:
            if d & bit:
                index = index + bit * (1 - 2 * ((lat // bit) % 2))
            bit *= 2
        return index

    def columns(q):
        low, high = chunk_tiles[q]
        return pl.ds(low * LANES, (high - low) * LANES)

    pending = []
    for q in range(3):
        for k in range(*chunk_loads[q]):
            loads[k].wait()
        low, high = chunk_tiles[q]
        spectra = jnp.dot(
            grid[pl.ds(low * LANES, (high - low) * LANES), :], twiddle[...],
            preferred_element_type=jnp.float32,
        )
        spectra = (spectra * (1.0 / lon_total)).astype(jnp.bfloat16)
        for t in range(low, high):
            part = spectra[(t - low) * LANES:(t - low + 1) * LANES, :]
            part = jnp.dot(order, part, preferred_element_type=jnp.float32)
            part = part.T
            for owner in range(lat_count):
                s0 = owner * slot_dev
                send[owner, :, pl.ds(t * LANES, LANES)] = jnp.concatenate(
                    [part[s0:s0 + slot_dev], part[slot_total + s0:slot_total + s0 + slot_dev]], axis=0
                ).astype(jnp.bfloat16)
        if q == 0:
            pl.semaphore_wait(barrier, lat_count + 1)
        for d in offsets:
            owner = flipped(d)
            copy = pltpu.make_async_remote_copy(
                src_ref=send.at[owner, :, columns(q)],
                dst_ref=recv.at[fld, lat, :, columns(q)],
                send_sem=send_sem.at[d, q],
                recv_sem=recv_sem.at[d, q],
                device_id=(owner, fld),
                device_id_type=MESH,
            )
            copy.start()
            pending.append(copy)
        for other, ss, rs in ((y_peer, y_send, y_recv), (partner, c_send, c_recv)):
            copy = pltpu.make_async_remote_copy(
                src_ref=send.at[lat, :, columns(q)],
                dst_ref=recv.at[fld, lat, :, columns(q)],
                send_sem=ss.at[0, q],
                recv_sem=rs.at[0, q],
                device_id=(lat, other),
                device_id_type=MESH,
            )
            copy.start()
            pending.append(copy)
        recv[fld, lat, :, columns(q)] = send[lat, :, columns(q)]

    table_copy = pltpu.make_async_copy(legendre_ref, table, table_sem)
    table_copy.start()

    for q in range(3):
        for d in near:
            src = flipped(d)
            here = recv.at[fld, src, :, columns(q)]
            pltpu.make_async_remote_copy(
                src_ref=here, dst_ref=here, send_sem=send_sem.at[d, q], recv_sem=recv_sem.at[d, q],
                device_id=(lat, y_peer), device_id_type=MESH,
            ).wait_recv()
            for other, ss, rs in ((y_peer, y_send, y_recv), (partner, c_send, c_recv)):
                copy = pltpu.make_async_remote_copy(
                    src_ref=here, dst_ref=here, send_sem=ss.at[d, q], recv_sem=rs.at[d, q],
                    device_id=(lat, other), device_id_type=MESH,
                )
                copy.start()
                pending.append(copy)
    for q in range(3):
        for d in [0] + near:
            src = flipped(d)
            there = recv.at[y_peer, src, :, columns(q)]
            pltpu.make_async_remote_copy(
                src_ref=there, dst_ref=there, send_sem=y_send.at[d, q], recv_sem=y_recv.at[d, q],
                device_id=(lat, y_peer), device_id_type=MESH,
            ).wait_recv()
            copy = pltpu.make_async_remote_copy(
                src_ref=there, dst_ref=there, send_sem=d_send.at[d, q], recv_sem=d_recv.at[d, q],
                device_id=(lat, partner), device_id_type=MESH,
            )
            copy.start()
            pending.append(copy)
    for q in range(3):
        for d in [0] + near:
            src = flipped(d)
            for group, ss, rs in ((partner, c_send, c_recv), (partner_y, d_send, d_recv)):
                place = recv.at[group, src, :, columns(q)]
                pltpu.make_async_remote_copy(
                    src_ref=place, dst_ref=place, send_sem=ss.at[d, q], recv_sem=rs.at[d, q],
                    device_id=(lat, partner), device_id_type=MESH,
                ).wait_recv()

    depth = 2 * slot_dev
    pair_lats = 2 * lat_dev
    low_half = lax.broadcasted_iota(jnp.int32, (depth, LANES), 1) < HALF
    for h in range(half_lats // 2):
        for group in range(4):
            north = [recv[group, 2 * h + o].astype(jnp.float32) for o in range(2)]
            mirror = [recv[group, lat_count - 1 - 2 * h - o].astype(jnp.float32) for o in range(2)]
            for p in range(2):
                even_band, odd_band = [
                    n + m if p == 0 else n - m for n, m in zip(north, mirror)
                ]
                cut = main * LANES
                mid_even = even_band[:, cut:cut + LANES]
                mid_odd = odd_band[:, cut:cut + LANES]
                mid = (
                    jnp.where(low_half, mid_even, mid_odd),
                    pltpu.roll(jnp.where(low_half, mid_odd, mid_even), HALF, 1),
                )
                for f in range(2):
                    start = f * (cut + LANES)
                    rows = pl.ds((2 * group + f) * depth, depth)
                    base = h * pair_lats
                    folded[p, rows, pl.ds(base, cut)] = even_band[:, start:start + cut].astype(jnp.bfloat16)
                    folded[p, rows, pl.ds(base + cut, LANES)] = mid[f].astype(jnp.bfloat16)
                    folded[p, rows, pl.ds(base + cut + LANES, cut)] = odd_band[
                        :, start:start + cut
                    ].astype(jnp.bfloat16)

    table_copy.wait()
    total_rows = 8 * depth
    trunc_total = 2 * row_dev * 4
    slot_of = lax.broadcasted_iota(jnp.int32, (row_dev, total_rows), 1) % slot_dev
    degree_row = 2 * (lax.broadcasted_iota(jnp.int32, (row_dev, total_rows), 0) + fld * row_dev)
    for p in range(2):
        kept = jnp.zeros((row_dev, total_rows), jnp.float32)
        for s in range(slot_dev):
            sums = lax.dot_general(
                table[s, p], folded[p], (((1,), (1,)), ((), ())), preferred_element_type=jnp.float32
            )
            wave = wave_scalar_ref[lat * slot_dev + s]
            valid = (slot_of == s) & (degree_row + (wave + p) <= trunc_total - 1)
            kept = jnp.where(valid, sums, kept)
        padded = jnp.concatenate(
            [kept, jnp.zeros((spun.shape[1] * LANES - row_dev, total_rows), jnp.float32)], axis=0
        )
        for t in range(spun.shape[1]):
            spun[p, t] = padded[t * LANES:(t + 1) * LANES].T
    for s in range(slot_dev):
        for p in range(2):
            for c in range(2):
                for t in range(spun.shape[1]):
                    kept_rows = min(LANES, row_dev - t * LANES)
                    out_ref[s, pl.ds(p * 16 + c * 8, 8), pl.ds(t * LANES, kept_rows)] = spun[
                        p, t, pl.ds(c * slot_dev + s, 8, stride=depth), :
                    ][:, :kept_rows]
    for copy in pending:
        copy.wait_send()


def shards_by_kernel(field_grid, wave_table, legendre):
    f_dev, lat_dev, lon_total = field_grid.shape
    slot_dev, _, row_dev, north_total = legendre.shape
    slot_total = wave_table.shape[0]
    lat_count = lax.axis_size("lat")
    rows = f_dev * lat_dev
    bf16, f32 = jnp.bfloat16, jnp.float32
    dma = pltpu.SemaphoreType.DMA
    padded_rows = -(-row_dev // LANES) * LANES
    coarse_rows = -(-(lon_total // LANES) // 8) * 8
    vmem, smem = pltpu.VMEM, pltpu.SMEM
    pairs = (lat_count, 3)
    out = pl.pallas_call(
        functools.partial(transform_kernel, lat_count),
        out_shape=pltpu.VMEM((slot_dev, 32, row_dev), f32),
        in_specs=[
            pl.BlockSpec(memory_space=smem),
            pl.BlockSpec(memory_space=vmem),
            pl.BlockSpec(memory_space=pl.ANY),
            pl.BlockSpec(memory_space=pl.ANY),
        ],
        out_specs=pl.BlockSpec(memory_space=vmem),
        scratch_shapes=[
            vmem((rows, lon_total), bf16),
            vmem((lon_total, 2 * slot_total), bf16),
            vmem((2, coarse_rows, 2 * slot_total), f32),
            vmem(legendre.shape, bf16),
            vmem((lat_count, 2 * slot_dev, rows), bf16),
            vmem((4, lat_count, 2 * slot_dev, rows), bf16),
            vmem((2, 16 * slot_dev, north_total), bf16),
            vmem((2, padded_rows // LANES, 16 * slot_dev, LANES), f32),
            dma((2 * (lat_dev // LANES) + 2,)),
            dma(()),
        ] + [dma(pairs)] * 8,
        compiler_params=pltpu.CompilerParams(
            collective_id=0, has_side_effects=True
        ),
    )(wave_table, wave_table.reshape(1, slot_total), field_grid, legendre)
    return jnp.transpose(out, (0, 2, 1))


def shards(field_grid, wave_table, legendre):
    f_dev, lat_dev, lon_total = field_grid.shape
    slot_dev, _, row_dev, _ = legendre.shape
    slot_total = wave_table.shape[0]
    fits = (
        f_dev == 2
        and slot_dev == 8
        and 2 * slot_total == LANES
        and lat_dev % LANES == HALF
        and lax.axis_size("fld") == 4
        and lax.axis_size("lat") in (4, 8, 16)
        and lon_total % LANES == 0
        and row_dev % 8 == 0
        and 2 * row_dev * 4 * lon_total < 2**24
    )
    if fits:
        return shards_by_kernel(field_grid, wave_table, legendre)
    return shards_by_collectives(field_grid, wave_table, legendre)


def solution(mesh):
    placed = (P("fld", "lat", None), P(), P("lat", None, "fld", None))
    return jax.shard_map(
        shards, mesh=mesh, in_specs=placed, out_specs=P("lat", "fld", None), check_vma=False
    )
```
